32 devices in a mesh: basis: 16 (over z, y, x), ex: 2 (over core).
Axes of the slice: x: 2, y: 2, z: 4, core: 2. Of those that a mesh axis runs over, the one named last changes fastest.
Arguments:
- activations: bfloat16 [64, 768, 2880], P(('basis', 'ex')), may hold values from -6 to 6
- out_grads: bfloat16 [64, 768, 2880], P(('basis', 'ex')), may hold values from -0.25 to 0.25
- grad_basis: bfloat16 [2880, 256], replicated, may hold values from -0.109375 to 0.109375
- panel_store: bfloat16 [16, 4, 2880, 128], P('basis', None, 'ex'), may hold values from -0.109375 to 0.109375
- owners: int32 [4], replicated, may hold values from 0 to 15, as said below
- token_count: int32 [64], P(('basis', 'ex')), may hold values from 96 to 768, as said below
Outputs:
- scaled: float32 [64, 256, 512], P('basis', 'ex')
The draws below stay inside these ranges and needn't reach their ends.
Inputs may be any that keep to these rules, and one draw needn't show every extreme that they name: `owners`: values are basis indices; panels may share an owner. `token_count`: some example has all 768 tokens live.
All inputs are finite; a program needn't handle non-finite values.
Results may differ from the reference program's by a relative error of at most 0.00045.
The reference program's roundings to bfloat16 on the way (of `in_basis`, `rot_act` and `rot_grad`) count: a program that leaves them out, or rounds other values in their place, can miss the bound.
Values may be sent and summed in bfloat16 or wider, within the bound.
A program may use at most 128 MiB of HBM per device.

```python
import jax
import jax.numpy as jnp
from jax import lax

D_IN = 2880
D_OUT = 2880
TOK = 768
PANEL = 128
PANELS = 4
DIRS = 256
EXAMPLES = 64
N_BASIS = 16


def draw_owners(key, part):
    first, second = jax.random.split(jax.random.fold_in(key, 11))
    picks = jax.random.randint(first, (PANELS,), 0, N_BASIS)
    picks = picks.at[0].set(0).at[1].set(N_BASIS - 1)
    return jax.random.permutation(second, picks).astype(jnp.int32)


def draw_token_count(key, part):
    first, second = jax.random.split(jax.random.fold_in(key, 23))
    counts = jax.random.randint(first, (EXAMPLES,), TOK // 8, TOK + 1)
    target = jax.random.randint(second, (), 0, EXAMPLES)
    return counts.at[target].set(TOK).astype(jnp.int32)


def steps_of(stream_key, dims, cuts, low, largest):
    def one(axis_at, shards_of):
        heights = jax.random.uniform(jax.random.fold_in(jax.random.fold_in(stream_key, 6), axis_at), (shards_of,), jnp.float32, low / len(cuts), largest / len(cuts))
        return jnp.repeat(jnp.exp(heights), dims[axis_at] // shards_of).reshape((-1,) + (1,) * (len(dims) - axis_at - 1))

    gain = one(*cuts[0])
    for cut in cuts[1:]:
        gain = gain * one(*cut)
    return gain


def normal_values(rng, shape, deviation, limit, cuts=(), dtype=jnp.bfloat16):
    result = deviation * jax.random.normal(rng, shape, jnp.float32)
    if cuts:
        result = result * steps_of(rng, shape, cuts, -0.22, 0.18)
    return jnp.clip(result, -limit, limit).astype(dtype)


def setup_inputs(seed: int = 0) -> dict:
    streams_of = jax.random.split(jax.random.key(seed), 7)
    activations = normal_values(streams_of[0], (EXAMPLES, TOK, D_IN), 1.0, 6.0, ((0, 32),))
    out_grads = normal_values(streams_of[1], (EXAMPLES, TOK, D_OUT), 0.036, 0.25, ((0, 32),))
    grad_basis = normal_values(streams_of[2], (D_OUT, DIRS), D_OUT ** -0.5, 0.109375)
    panel_store = normal_values(streams_of[3], (N_BASIS, PANELS, D_IN, PANEL), D_IN ** -0.5, 0.109375, ((0, 16), (2, 2)))
    owners = draw_owners(jax.random.fold_in(streams_of[6], 71), 0)
    token_count = draw_token_count(jax.random.fold_in(streams_of[6], 71), 0)
    return {"activations": activations, "out_grads": out_grads, "grad_basis": grad_basis, "panel_store": panel_store, "owners": owners, "token_count": token_count}


def reference(activations, out_grads, grad_basis, panel_store, owners, token_count):
    picked = panel_store[owners, jnp.arange(PANELS)]
    in_basis = jnp.transpose(picked, (1, 0, 2)).reshape(D_IN, PANELS * PANEL)
    positions = jnp.arange(TOK)

    def one_example(inputs):
        act_rows, grad_rows, length = inputs
        rot_act = jnp.dot(act_rows, in_basis, preferred_element_type=jnp.float32).astype(jnp.bfloat16)
        rot_grad = jnp.dot(grad_rows, grad_basis, preferred_element_type=jnp.float32).astype(jnp.bfloat16)
        rot_grad = jnp.where((positions < length)[:, None], rot_grad, jnp.zeros((), jnp.bfloat16))
        return jnp.dot(rot_grad.T, rot_act, preferred_element_type=jnp.float32)

    ex_grads = lax.map(one_example, (activations, out_grads, token_count))
    lambdas = jnp.sum(ex_grads * ex_grads, axis=0) / EXAMPLES
    damp = 0.1 * jnp.mean(lambdas)
    return ex_grads / (lambdas + damp)
```

```python
import functools

import jax
import jax.numpy as jnp
from jax import lax
from jax.experimental import pallas as pl
from jax.experimental.pallas import tpu as pltpu
from jax.sharding import PartitionSpec as P

MESH = pl.DeviceIdType.MESH
LANE = 128
CHUNK = 256


def round_up(value, unit):
    return -(-value // unit) * unit


def split_kinds(rows, lanes, bits, row_unit):
    kinds = []
    for _ in range(bits):
        if (lanes // 2) % LANE == 0:
            kinds.append("lane")
            lanes //= 2
        elif (rows // 2) % row_unit == 0:
            kinds.append("row")
            rows //= 2
        else:
            return None
    return kinds


class Exchange:
    def __init__(self, base, rows, lanes, order, row_unit, basis, ex):
        self.order = order
        kinds = split_kinds(rows, lanes, len(order), row_unit)
        r0, l0 = 0, 0
        self.kept, self.sent, self.partner = [], [], []
        for kind, bit in zip(kinds, order):
            mine = (basis // (1 << bit)) % 2
            self.partner.append((basis + (1 - 2 * mine) * (1 << bit), ex))
            if kind == "lane":
                lanes //= 2
                self.kept.append((r0, rows, l0 + mine * lanes, lanes))
                self.sent.append((r0, rows, l0 + (1 - mine) * lanes, lanes))
            else:
                rows //= 2
                self.kept.append((r0 + mine * rows, rows, l0, lanes))
                self.sent.append((r0 + (1 - mine) * rows, rows, l0, lanes))
            r0, _, l0, _ = self.kept[-1]
        self.base = base
        self.row_unit = row_unit

    def at(self, region):
        r0, rows, l0, lanes = region
        row_start = self.base[0] + r0
        lane_start = self.base[1] + l0
        if not isinstance(row_start, int):
            row_start = pl.multiple_of(row_start, self.row_unit)
        if not isinstance(lane_start, int):
            lane_start = pl.multiple_of(lane_start, LANE)
        return pl.ds(row_start, rows), pl.ds(lane_start, lanes)


def stage_shapes(rows, lanes, bits, row_unit):
    shapes = []
    for kind in split_kinds(rows, lanes, bits, row_unit):
        if kind == "lane":
            lanes //= 2
        else:
            rows //= 2
        shapes.append((rows, lanes))
    return shapes


def kernel(
    cfg,
    owners_ref, count_ref, store_ref, gb_ref, act_ref, go_ref,
    out_ref,
    slots, gbv, gbt, act, go, work, full, acc, rot_g, rot_a, exg, exr, lam, lam_full, tot, tot_in,
    *rest,
):
    bits, n_ex, n_panels, half_rows, pad_rows, in_w, go_w, go_pad, tok, dirs, lam_parts = cfg
    recv = rest[:bits]
    lam_recv = rest[bits : 2 * bits]
    (store_sem, gb_sem, act_sem, go_sem, rs_s, rs_r, ag_s, ag_r, sb_s, sb_r,
     eg_s, eg_r, ls_s, ls_r, lg_s, lg_r, ts_s, ts_r) = rest[2 * bits :]
    basis = lax.axis_index("basis")
    ex = lax.axis_index("ex")
    sibling = (basis, 1 - ex)
    sends = []

    def remote(src, dst, s_sem, r_sem, to):
        copy = pltpu.make_async_remote_copy(
            src_ref=src, dst_ref=dst, send_sem=s_sem, recv_sem=r_sem, device_id=to, device_id_type=MESH
        )
        return copy

    def launch(copy):
        copy.start()
        sends.append(copy)
        return copy

    barrier = pltpu.get_barrier_semaphore()
    pl.semaphore_signal(barrier, inc=1, device_id=sibling, device_id_type=MESH)
    for bit in range(bits):
        mine = (basis // (1 << bit)) % 2
        peer = basis + (1 - 2 * mine) * (1 << bit)
        pl.semaphore_signal(barrier, inc=1, device_id=(peer, ex), device_id_type=MESH)

    half_panels = n_panels // 2
    issue = []
    for p in range(half_panels):
        issue += [p, p + half_panels]
    issue += [p for p in range(n_panels) if p not in issue]
    store_in = []
    for p in range(n_panels):
        store_in.append(pltpu.make_async_copy(
            store_ref.at[0, p], slots.at[p, pl.ds(0, half_rows)], store_sem.at[p]))
    for p in issue:
        store_in[p].start()
    gb_in = pltpu.make_async_copy(gb_ref, gbv.at[pl.ds(0, go_w)], gb_sem)
    gb_in.start()
    go_in = [pltpu.make_async_copy(go_ref.at[n], go.at[n, pl.ds(0, go_w)], go_sem.at[n]) for n in range(n_ex)]
    act_in = [pltpu.make_async_copy(act_ref.at[n], act.at[n, pl.ds(0, in_w)], act_sem.at[n]) for n in range(n_ex)]
    for copy in go_in + act_in:
        copy.start()

    first = list(range(bits))
    second = [1, 0] + first[2:] if bits > 1 else first
    parts = [
        Exchange((p * LANE, 0), LANE, pad_rows, first if p < half_panels else second, 16, basis, ex)
        for p in range(n_panels)
    ]

    if pad_rows > half_rows:
        for p in range(n_panels):
            slots[p, pl.ds(half_rows, pad_rows - half_rows), :] = jnp.zeros(
                (pad_rows - half_rows, LANE), slots.dtype)

    def rs_copy(p, j):
        return remote(work.at[parts[p].at(parts[p].sent[j])], recv[j].at[p],
                      rs_s.at[p, j], rs_r.at[p, j], parts[p].partner[j])

    rs = {}
    for i, p in enumerate(issue):
        store_in[p].wait()
        own = owners_ref[p] == basis
        for kb in range(pad_rows // LANE):
            block = slots[p, pl.ds(kb * LANE, LANE), :]
            block = jnp.where(own, block, jnp.zeros_like(block))
            work[pl.ds(p * LANE, LANE), pl.ds(kb * LANE, LANE)] = block.T
        if i == 0:
            pl.semaphore_wait(barrier, bits + 1)
        rs[p, 0] = launch(rs_copy(p, 0))

    gb_in.wait()
    if go_pad > go_w:
        gbv[pl.ds(go_w, go_pad - go_w), :] = jnp.zeros((go_pad - go_w, dirs), gbv.dtype)
        for n in range(n_ex):
            go[n, pl.ds(go_w, go_pad - go_w), :] = jnp.zeros((go_pad - go_w, tok), go.dtype)
    tail = act.shape[1] - in_w
    if tail > 0:
        for n in range(n_ex):
            act[n, pl.ds(in_w, tail), :] = jnp.zeros((tail, tok), act.dtype)
    for kb in range(go_pad // LANE):
        for db in range(dirs // LANE):
            gbt[pl.ds(db * LANE, LANE), pl.ds(kb * LANE, LANE)] = gbv[
                pl.ds(kb * LANE, LANE), pl.ds(db * LANE, LANE)].T

    go_ready = [False] * n_ex

    def rotate_grads(n, t):
        if not go_ready[n]:
            go_in[n].wait()
            go_ready[n] = True
        value = jnp.dot(gbt[...], go[n, :, pl.ds(t, CHUNK)], preferred_element_type=jnp.float32)
        value = value.astype(jnp.bfloat16)
        at = lax.broadcasted_iota(jnp.int32, value.shape, 1) + t
        rot_g[n, :, pl.ds(t, CHUNK)] = jnp.where(at < count_ref[n], value, jnp.zeros_like(value))

    jobs = [(n, t) for n in range(n_ex) for t in range(0, tok, CHUNK)]

    def some_jobs(number):
        for _ in range(min(number, len(jobs))):
            rotate_grads(*jobs.pop(0))

    def ag_copy(p, j):
        where = (ex,) + parts[p].at(parts[p].kept[j])
        return remote(full.at[where], full.at[where], ag_s.at[p, j], ag_r.at[p, j], parts[p].partner[j])

    def sb_copy(p, j):
        region = parts[p].kept[bits - 1] if j == bits else parts[p].sent[j]
        where = (ex,) + parts[p].at(region)
        return remote(full.at[where], full.at[where], sb_s.at[p, j], sb_r.at[p, j], sibling)

    def sb_wait(p, j):
        region = parts[p].kept[bits - 1] if j == bits else parts[p].sent[j]
        where = (1 - ex,) + parts[p].at(region)
        remote(full.at[where], full.at[where], sb_s.at[p, j], sb_r.at[p, j], sibling).wait_recv()

    ag = {}
    for j in range(bits):
        some_jobs(1)
        for p in issue:
            rs[p, j].wait_recv()
            kept = parts[p].at(parts[p].kept[j])
            total = work[kept] + recv[j][p]
            if j + 1 < bits:
                work[kept] = total
                rs[p, j + 1] = launch(rs_copy(p, j + 1))
            else:
                full[(ex,) + kept] = total
                ag[p, j] = launch(ag_copy(p, j))
                launch(sb_copy(p, bits))

    for j in range(bits - 1, 0, -1):
        some_jobs(1)
        for p in issue:
            ag[p, j].wait_recv()
            ag[p, j - 1] = launch(ag_copy(p, j - 1))
            launch(sb_copy(p, j))
    some_jobs(len(jobs))
    for copy in act_in:
        copy.wait()

    half_k = pad_rows // 2
    pair_rows = half_panels * LANE

    def rotate_acts(pair, other, side, stage):
        bit = parts[pair * half_panels].order[0]
        mine = (basis // (1 << bit)) % 2
        pick = 1 - mine if other else mine
        k_at = pl.multiple_of(pick * half_k, LANE)
        row_at = pl.multiple_of(side * half_rows + pick * half_k, 16)
        rows = pl.ds(pair * pair_rows, pair_rows)
        lhs = full[side, rows, pl.ds(k_at, half_k)]
        for n in range(n_ex):
            for t in range(0, tok, CHUNK):
                value = jnp.dot(lhs, act[n, pl.ds(row_at, half_k), pl.ds(t, CHUNK)],
                                preferred_element_type=jnp.float32)
                cols = pl.ds(t, CHUNK)
                if stage > 0:
                    value = value + acc[n, rows, cols]
                if stage == 2:
                    rot_a[n, rows, cols] = value.astype(jnp.bfloat16)
                else:
                    acc[n, rows, cols] = value

    members = [issue_p for issue_p in ([p for p in issue if p < half_panels],
                                       [p for p in issue if p >= half_panels])]
    for pair in range(2):
        rotate_acts(pair, False, ex, 0)
    for pair in range(2):
        for p in members[pair]:
            for j in range(bits, 0, -1):
                sb_wait(p, j)
        rotate_acts(pair, False, 1 - ex, 1)
    for p in issue:
        ag[p, 0].wait_recv()
        launch(sb_copy(p, 0))
    for pair in range(2):
        rotate_acts(pair, True, ex, 1)
    for pair in range(2):
        for p in members[pair]:
            sb_wait(p, 0)
        rotate_acts(pair, True, 1 - ex, 2)

    share = dirs // 2
    theirs = pl.ds(pl.multiple_of((1 - ex) * share, 8), share)
    ours = pl.ds(pl.multiple_of(ex * share, 8), share)
    eg = []
    tile_sum = jnp.zeros((8, LANE), jnp.float32)
    for n in range(n_ex):
        value = lax.dot_general(rot_g[n], rot_a[n], (((1,), (1,)), ((), ())),
                                preferred_element_type=jnp.float32)
        exg[n] = value
        eg.append(launch(remote(exg.at[n, theirs], exr.at[n], eg_s.at[n], eg_r.at[n], sibling)))
        squares = value * value
        columns = squares[:, :LANE]
        for c in range(LANE, squares.shape[1], LANE):
            columns = columns + squares[:, c : c + LANE]
        tile_sum = tile_sum + jnp.sum(columns.reshape(dirs // 8, 8, LANE), axis=0)
    tot[0] = tile_sum

    def tot_copy(j):
        if j == 0:
            to = sibling
        else:
            to = lam_ex[0].partner[j - 1]
        return remote(tot.at[j], tot_in.at[j], ts_s.at[j], ts_r.at[j], to)

    width = lam.shape[1]
    lam_lanes = width // lam_parts
    lam_ex = [
        Exchange((0, c * lam_lanes), share, lam_lanes, first if c == 0 else second, 8, basis, ex)
        for c in range(lam_parts)
    ]
    tots = [launch(tot_copy(0))]
    for copy in eg:
        copy.wait_recv()
    partial = jnp.zeros((share, width), jnp.float32)
    for n in range(n_ex):
        here, there = exg[n, ours, :], exr[n]
        partial = partial + (here * here + there * there)
    lam[...] = partial

    def ls_copy(c, j):
        return remote(lam.at[lam_ex[c].at(lam_ex[c].sent[j])], lam_recv[j].at[c],
                      ls_s.at[c, j], ls_r.at[c, j], lam_ex[c].partner[j])

    def lg_copy(c, j):
        where = lam_ex[c].at(lam_ex[c].kept[j])
        return remote(lam_full.at[where], lam_full.at[where], lg_s.at[c, j], lg_r.at[c, j],
                      lam_ex[c].partner[j])

    def next_total(j):
        tots[j].wait_recv()
        tot[j + 1] = tot[j] + tot_in[j]

    ls, lg = {}, {}
    for c in range(lam_parts):
        ls[c, 0] = launch(ls_copy(c, 0))
    next_total(0)
    tots.append(launch(tot_copy(1)))
    for j in range(bits):
        for c in range(lam_parts):
            ls[c, j].wait_recv()
            kept = lam_ex[c].at(lam_ex[c].kept[j])
            total = lam[kept] + lam_recv[j][c]
            if j + 1 < bits:
                lam[kept] = total
                ls[c, j + 1] = launch(ls_copy(c, j + 1))
            else:
                lam_full[kept] = total
                lg[c, j] = launch(lg_copy(c, j))
        next_total(j + 1)
        if j + 1 < bits:
            tots.append(launch(tot_copy(j + 2)))
    for j in range(bits - 1, 0, -1):
        for c in range(lam_parts):
            lg[c, j].wait_recv()
            lg[c, j - 1] = launch(lg_copy(c, j - 1))
    ex_count = n_ex * 2 * (1 << bits)
    damp = 0.1 * (jnp.sum(tot[bits + 1], keepdims=True) / ex_count / (dirs * width))
    for c in range(lam_parts):
        lg[c, 0].wait_recv()
    scale = lam_full[...] / ex_count + damp
    for n in range(n_ex):
        out_ref[ex * n_ex + n] = exg[n, ours, :] / scale
        out_ref[(1 - ex) * n_ex + n] = exr[n] / scale
    for copy in sends:
        copy.wait_send()


def per_device(activations, out_grads, grad_basis, panel_store, owners, token_count):
    n_ex, tok, in_w = activations.shape
    go_w = out_grads.shape[2]
    dirs = grad_basis.shape[1]
    _, n_panels, half_rows, panel = panel_store.shape
    n_basis = lax.axis_size("basis")
    bits = n_basis.bit_length() - 1
    assert 1 << bits == n_basis and lax.axis_size("ex") == 2
    pad_rows = round_up(half_rows, 2 * LANE)
    while split_kinds(panel, pad_rows, bits, 16) is None:
        pad_rows += 2 * LANE
    go_pad = round_up(go_w, LANE)
    act_rows = max(in_w, half_rows + pad_rows)
    width = n_panels * panel
    share = dirs // 2
    lam_parts = 2 if split_kinds(share, width // 2, bits, 8) else 1
    cfg = (bits, n_ex, n_panels, half_rows, pad_rows, in_w, go_w, go_pad, tok, dirs, lam_parts)
    bf16, f32 = jnp.bfloat16, jnp.float32
    dma = pltpu.SemaphoreType.DMA
    scratch = [
        pltpu.VMEM((n_panels, pad_rows, panel), bf16),
        pltpu.VMEM((go_pad, dirs), bf16),
        pltpu.VMEM((dirs, go_pad), bf16),
        pltpu.VMEM((n_ex, act_rows, tok), bf16),
        pltpu.VMEM((n_ex, go_pad, tok), bf16),
        pltpu.VMEM((width, pad_rows), bf16),
        pltpu.VMEM((2, width, pad_rows), bf16),
        pltpu.VMEM((n_ex, width, tok), f32),
        pltpu.VMEM((n_ex, dirs, tok), bf16),
        pltpu.VMEM((n_ex, width, tok), bf16),
        pltpu.VMEM((n_ex, dirs, width), f32),
        pltpu.VMEM((n_ex, share, width), f32),
        pltpu.VMEM((share, width), f32),
        pltpu.VMEM((share, width), f32),
        pltpu.VMEM((bits + 2, 8, LANE), f32),
        pltpu.VMEM((bits + 1, 8, LANE), f32),
    ]
    for rows, lanes in stage_shapes(panel, pad_rows, bits, 16):
        scratch.append(pltpu.VMEM((n_panels, rows, lanes), bf16))
    for rows, lanes in stage_shapes(share, width // lam_parts, bits, 8):
        scratch.append(pltpu.VMEM((lam_parts, rows, lanes), f32))
    scratch += [dma((n_panels,)), dma, dma((n_ex,)), dma((n_ex,))]
    scratch += [dma((n_panels, bits))] * 4 + [dma((n_panels, bits + 1))] * 2
    scratch += [dma((n_ex,))] * 2 + [dma((lam_parts, bits))] * 4 + [dma((bits + 1,))] * 2
    smem = pl.BlockSpec(memory_space=pltpu.SMEM)
    anywhere = pl.BlockSpec(memory_space=pl.ANY)
    return pl.pallas_call(
        functools.partial(kernel, cfg),
        out_shape=jax.ShapeDtypeStruct((2 * n_ex, share, width), f32),
        in_specs=[smem, smem, anywhere, anywhere, anywhere, anywhere],
        out_specs=pl.BlockSpec(memory_space=pltpu.VMEM),
        scratch_shapes=scratch,
        compiler_params=pltpu.CompilerParams(
            collective_id=0, has_side_effects=True, vmem_limit_bytes=60 * 1024 * 1024),
        name="ekfac",
    )(owners, token_count, panel_store, grad_basis,
      jnp.swapaxes(activations, 1, 2), jnp.swapaxes(out_grads, 1, 2))


def solution(mesh):
    return jax.shard_map(
        per_device,
        mesh=mesh,
        in_specs=(
            P(("basis", "ex"), None, None),
            P(("basis", "ex"), None, None),
            P(),
            P("basis", None, "ex", None),
            P(),
            P(("basis", "ex")),
        ),
        out_specs=P("basis", "ex", None),
        check_vma=False,
    )
```

```python
import functools

import jax
import jax.numpy as jnp
from jax import lax
from jax.experimental import pallas as pl
from jax.experimental.pallas import tpu as pltpu
from jax.sharding import PartitionSpec as P

MESH = pl.DeviceIdType.MESH
LANE = 128
CHUNK = 256


def round_up(value, unit):
    return -(-value // unit) * unit


class Quarter:
    def __init__(self, base, rows, lanes, order, basis, ex):
        self.kept, self.sent, self.partner = [], [], []
        at = 0
        for bit in order:
            mine = (basis // (1 << bit)) % 2
            lanes //= 2
            self.partner.append((basis + (1 - 2 * mine) * (1 << bit), ex))
            self.kept.append((base, rows, at + mine * lanes, lanes))
            self.sent.append((base, rows, at + (1 - mine) * lanes, lanes))
            at = at + mine * lanes


def window(region):
    base, rows, at, lanes = region
    return pl.ds(base, rows), pl.ds(pl.multiple_of(at, LANE), lanes)


def kernel(
    cfg,
    owners_ref, count_ref, store_ref, gb_ref, act_ref, go_ref,
    out_ref,
    slots, gbv, gbt, act, go, work, full, acc, rot_g, rot_a, exg, exr,
    in0, in1, own, up_in, up_out, down_in, down_out,
    lam, lam_in1, lam_mid, lam_in2, lam_full, tot, tot_sib, tot_in1, tot_in2,
    store_sem, gb_sem, act_sem, go_sem, rs_s, rs_r, ag_s, ag_r, sb_s, sb_r,
    up_s, up_r, dn_s, dn_r, eg_s, eg_r, l1_s, l1_r, l2_s, l2_r, l3_s, l3_r,
    t0_s, t0_r, t1_s, t1_r, t2_s, t2_r,
):
    n_basis, n_ex, n_panels, half_rows, pad_rows, in_w, go_w, go_pad, tok, dirs = cfg
    basis = lax.axis_index("basis")
    ex = lax.axis_index("ex")
    sibling = (basis, 1 - ex)
    levels = n_basis // 4
    quad = basis % 4
    level = basis // 4
    sends = []

    def quad_at(m):
        low, high = quad % 2, quad // 2
        low = 1 - low if m % 2 else low
        high = 1 - high if m // 2 else high
        return low + 2 * high

    quad_peers = {m: (level * 4 + quad_at(m), ex) for m in (1, 2, 3)}
    level_peers = {s: (((level + s) % levels) * 4 + quad, ex) for s in range(1, levels)}

    def remote(src, dst, s_sem, r_sem, to):
        return pltpu.make_async_remote_copy(
            src_ref=src, dst_ref=dst, send_sem=s_sem, recv_sem=r_sem, device_id=to, device_id_type=MESH
        )

    def launch(copy):
        copy.start()
        sends.append(copy)
        return copy

    barrier = pltpu.get_barrier_semaphore()
    greeted = [sibling] + list(quad_peers.values()) + list(level_peers.values())
    for peer in greeted:
        pl.semaphore_signal(barrier, inc=1, device_id=peer, device_id_type=MESH)

    groups = [[p, p + 1] for p in range(0, n_panels, 2)]
    store_in = []
    for p in range(n_panels):
        store_in.append(pltpu.make_async_copy(
            store_ref.at[0, p], slots.at[p, pl.ds(0, half_rows)], store_sem.at[p]))
        store_in[p].start()
    gb_in = pltpu.make_async_copy(gb_ref, gbv.at[pl.ds(0, go_w)], gb_sem)
    gb_in.start()
    go_in = [pltpu.make_async_copy(go_ref.at[n], go.at[n, pl.ds(0, go_w)], go_sem.at[n]) for n in range(n_ex)]
    act_in = [pltpu.make_async_copy(act_ref.at[n], act.at[n, pl.ds(0, in_w)], act_sem.at[n]) for n in range(n_ex)]
    for copy in go_in + act_in:
        copy.start()

    parts = [
        Quarter(p * LANE, LANE, pad_rows, (1, 0) if p % 2 else (0, 1), basis, ex) for p in range(n_panels)
    ]
    halves_in = (in0, in1)

    if pad_rows > half_rows:
        for p in range(n_panels):
            slots[p, pl.ds(half_rows, pad_rows - half_rows), :] = jnp.zeros(
                (pad_rows - half_rows, LANE), slots.dtype)

    def rs_copy(p, j):
        return remote(work.at[window(parts[p].sent[j])], halves_in[j].at[p],
                      rs_s.at[p, j], rs_r.at[p, j], parts[p].partner[j])

    def prepare(p):
        store_in[p].wait()
        mine = owners_ref[p] == basis
        for kb in range(pad_rows // LANE):
            block = slots[p, pl.ds(kb * LANE, LANE), :]
            block = jnp.where(mine, block, jnp.zeros_like(block))
            work[pl.ds(p * LANE, LANE), pl.ds(kb * LANE, LANE)] = block.T

    rs = {}

    def start_halving(group):
        for p in group:
            rs[p, 0] = launch(rs_copy(p, 0))

    def second_halving(group):
        for p in group:
            rs[p, 0].wait_recv()
            at = window(parts[p].kept[0])
            work[at] = work[at] + in0[p]
            rs[p, 1] = launch(rs_copy(p, 1))

    def up_copy(src, p):
        return remote(src.at[p], up_in.at[p], up_s.at[p], up_r.at[p], (basis + 4, ex))

    def down_copy(src, p):
        return remote(src.at[p], down_in.at[p], dn_s.at[p], dn_r.at[p], (basis - 4, ex))

    def start_scan(group):
        for p in group:
            rs[p, 1].wait_recv()
            at = window(parts[p].kept[1])
            value = work[at] + in1[p]
            own[p] = value
            full[(ex,) + at] = value

        if levels > 1:
            @pl.when(level == 0)
            def _():
                for p in group:
                    up_copy(own, p).start()

            @pl.when(level == levels - 1)
            def _():
                for p in group:
                    down_copy(own, p).start()

    def scan_round(group, r):
        def step(copy, arrived, onward, forward):
            for p in group:
                at = window(parts[p].kept[1])
                copy(own, p).wait_recv()
                if forward:
                    onward[p] = own[p] + arrived[p]
                    copy(onward, p).start()
                full[(ex,) + at] = full[(ex,) + at] + arrived[p]

        @pl.when(level == r + 1)
        def _():
            step(up_copy, up_in, up_out, r + 1 < levels - 1)

        @pl.when(level == levels - 2 - r)
        def _():
            step(down_copy, down_in, down_out, r + 1 < levels - 1)

    def finish_scan_sends():
        if levels == 1:
            return

        @pl.when(level < levels - 1)
        def _():
            for p in range(n_panels):
                up_copy(own, p).wait_send()

        @pl.when(level > 0)
        def _():
            for p in range(n_panels):
                down_copy(own, p).wait_send()

    def ag_copy(p, j):
        where = (ex,) + window(parts[p].kept[j])
        return remote(full.at[where], full.at[where], ag_s.at[p, j], ag_r.at[p, j], parts[p].partner[j])

    def sb_copy(p, j, side):
        region = parts[p].kept[1] if j == 2 else parts[p].sent[j]
        where = (side,) + window(region)
        return remote(full.at[where], full.at[where], sb_s.at[p, j], sb_r.at[p, j], sibling)

    ag = {}

    def start_gather(group):
        for p in group:
            ag[p, 1] = launch(ag_copy(p, 1))
        for p in group:
            launch(sb_copy(p, 2, ex))

    def second_gather(group):
        for p in group:
            ag[p, 1].wait_recv()
            ag[p, 0] = launch(ag_copy(p, 0))
        for p in group:
            launch(sb_copy(p, 1, ex))

    def end_gather(group):
        for p in group:
            ag[p, 0].wait_recv()
            launch(sb_copy(p, 0, ex))

    def await_sibling(group):
        for j in (2, 1, 0):
            for p in group:
                sb_copy(p, j, 1 - ex).wait_recv()

    go_ready = [False] * n_ex

    def rotate_grads(n, t):
        if not go_ready[n]:
            go_in[n].wait()
            go_ready[n] = True
        value = jnp.dot(gbt[...], go[n, :, pl.ds(t, CHUNK)], preferred_element_type=jnp.float32)
        value = value.astype(jnp.bfloat16)
        at = lax.broadcasted_iota(jnp.int32, value.shape, 1) + t
        rot_g[n, :, pl.ds(t, CHUNK)] = jnp.where(at < count_ref[n], value, jnp.zeros_like(value))

    jobs = [(n, t) for n in range(n_ex) for t in range(0, tok, CHUNK)]

    def some_jobs(number):
        for _ in range(min(number, len(jobs))):
            rotate_grads(*jobs.pop(0))

    group_w = 2 * LANE

    def rotate_acts(g, side, last):
        rows = pl.ds(g * group_w, group_w)
        row_at = pl.multiple_of(side * half_rows, 16)
        for n in range(n_ex):
            for t in range(0, tok, CHUNK):
                cols = pl.ds(t, CHUNK)
                value = jnp.dot(full[side, rows, :], act[n, pl.ds(row_at, pad_rows), cols],
                                preferred_element_type=jnp.float32)
                if last:
                    rot_a[n, rows, cols] = (value + acc[n, :, cols]).astype(jnp.bfloat16)
                else:
                    acc[n, :, cols] = value

    share = dirs // 2
    part_rows = share // 4
    theirs = pl.ds(pl.multiple_of((1 - ex) * share, 8), share)
    ours = pl.ds(pl.multiple_of(ex * share, 8), share)
    eg = {}
    tile_sums = []

    def gradients(g):
        cols = pl.ds(g * group_w, group_w)
        for n in range(n_ex):
            value = lax.dot_general(rot_g[n], rot_a[n, cols, :], (((1,), (1,)), ((), ())),
                                    preferred_element_type=jnp.float32)
            exg[n, :, cols] = value
            eg[g, n] = launch(remote(exg.at[n, theirs, cols], exr.at[n, :, cols],
                                     eg_s.at[g, n], eg_r.at[g, n], sibling))
            squares = value * value
            columns = squares[:, :LANE] + squares[:, LANE:]
            tile_sums.append(jnp.sum(columns.reshape(dirs // 8, 8, LANE), axis=0))

    l1, l2, l3 = {}, {}, {}

    def quad_rows(index):
        return pl.ds(pl.multiple_of(index * part_rows, 8), part_rows)

    def lam_one(g):
        cols = pl.ds(g * group_w, group_w)
        partial = jnp.zeros((share, group_w), jnp.float32)
        for n in range(n_ex):
            eg[g, n].wait_recv()
            here, there = exg[n, ours, cols], exr[n, :, cols]
            partial = partial + (here * here + there * there)
        lam[g] = partial
        for m in (3, 1, 2):
            l1[g, m] = launch(remote(lam.at[g, quad_rows(quad_at(m))], lam_in1.at[g, m - 1],
                                     l1_s.at[g, m - 1], l1_r.at[g, m - 1], quad_peers[m]))

    def lam_two(g):
        total = lam[g, quad_rows(quad), :]
        for m in (1, 2, 3):
            l1[g, m].wait_recv()
            total = total + lam_in1[g, m - 1]
        lam_mid[g] = total
        for s in range(1, levels):
            l2[g, s] = launch(remote(lam_mid.at[g], lam_in2.at[g, s - 1],
                                     l2_s.at[g, s - 1], l2_r.at[g, s - 1], level_peers[s]))

    def lam_three(g):
        total = lam_mid[g]
        for s in range(1, levels):
            l2[g, s].wait_recv()
            total = total + lam_in2[g, s - 1]
        at = quad_rows(quad)
        lam_full[g, at, :] = total
        for m in (3, 1, 2):
            l3[g, m] = launch(remote(lam_full.at[g, at], lam_full.at[g, at],
                                     l3_s.at[g, m - 1], l3_r.at[g, m - 1], quad_peers[m]))

    def lam_end(g):
        for m in (1, 2, 3):
            l3[g, m].wait_recv()

    first, second = groups
    last_round = levels - 2
    for p in first:
        prepare(p)
    pl.semaphore_wait(barrier, len(greeted))
    start_halving(first)
    for p in second:
        prepare(p)
    gb_in.wait()
    if go_pad > go_w:
        gbv[pl.ds(go_w, go_pad - go_w), :] = jnp.zeros((go_pad - go_w, dirs), gbv.dtype)
        for n in range(n_ex):
            go[n, pl.ds(go_w, go_pad - go_w), :] = jnp.zeros((go_pad - go_w, tok), go.dtype)
    tail = act.shape[1] - in_w
    if tail > 0:
        for n in range(n_ex):
            act[n, pl.ds(in_w, tail), :] = jnp.zeros((tail, tok), act.dtype)
    for kb in range(go_pad // LANE):
        for db in range(dirs // LANE):
            gbt[pl.ds(db * LANE, LANE), pl.ds(kb * LANE, LANE)] = gbv[
                pl.ds(kb * LANE, LANE), pl.ds(db * LANE, LANE)].T
    second_halving(first)
    start_halving(second)
    some_jobs(2)
    start_scan(first)
    some_jobs(1)
    for r in range(levels - 1):
        scan_round(first, r)
        if r == 0:
            second_halving(second)
            some_jobs(1)
    start_gather(first)
    start_scan(second)
    some_jobs(1)
    for r in range(levels - 1):
        scan_round(second, r)
        if r == 0:
            second_gather(first)
            some_jobs(len(jobs))
    if levels == 1:
        second_halving(second)
        second_gather(first)
    start_gather(second)
    some_jobs(len(jobs))
    for copy in act_in:
        copy.wait()
    end_gather(first)
    second_gather(second)
    rotate_acts(0, ex, False)
    await_sibling(first)
    rotate_acts(0, 1 - ex, True)
    gradients(0)
    lam_one(0)
    end_gather(second)
    rotate_acts(1, ex, False)
    lam_two(0)
    await_sibling(second)
    rotate_acts(1, 1 - ex, True)
    gradients(1)
    lam_three(0)

    whole = tile_sums[0]
    for tile in tile_sums[1:]:
        whole = whole + tile
    tot[0] = whole
    t0 = launch(remote(tot.at[0], tot_sib, t0_s, t0_r, sibling))
    lam_one(1)
    t0.wait_recv()
    tot[1] = tot[0] + tot_sib[...]
    t1 = {m: launch(remote(tot.at[1], tot_in1.at[m - 1], t1_s.at[m - 1], t1_r.at[m - 1], quad_peers[m]))
          for m in (1, 2, 3)}
    lam_two(1)
    whole = tot[1]
    for m in (1, 2, 3):
        t1[m].wait_recv()
        whole = whole + tot_in1[m - 1]
    tot[2] = whole
    t2 = {s: launch(remote(tot.at[2], tot_in2.at[s - 1], t2_s.at[s - 1], t2_r.at[s - 1], level_peers[s]))
          for s in range(1, levels)}
    lam_three(1)
    whole = tot[2]
    for s in range(1, levels):
        t2[s].wait_recv()
        whole = whole + tot_in2[s - 1]
    ex_count = n_ex * 2 * n_basis
    width = n_panels * LANE
    damp = 0.1 * (jnp.sum(whole, keepdims=True) / ex_count / (dirs * width))
    for g in range(2):
        lam_end(g)
        cols = pl.ds(g * group_w, group_w)
        scale = lam_full[g] / ex_count + damp
        for n in range(n_ex):
            out_ref[ex * n_ex + n, :, cols] = exg[n, ours, cols] / scale
            out_ref[(1 - ex) * n_ex + n, :, cols] = exr[n, :, cols] / scale
    for copy in sends:
        copy.wait_send()
    finish_scan_sends()


def per_device(activations, out_grads, grad_basis, panel_store, owners, token_count):
    n_ex, tok, in_w = activations.shape
    go_w = out_grads.shape[2]
    dirs = grad_basis.shape[1]
    _, n_panels, half_rows, panel = panel_store.shape
    n_basis = lax.axis_size("basis")
    assert n_basis % 4 == 0 and lax.axis_size("ex") == 2 and n_panels == 4 and panel == LANE
    pad_rows = round_up(half_rows, 4 * LANE)
    go_pad = round_up(go_w, LANE)
    act_rows = max(in_w, half_rows + pad_rows)
    width = n_panels * panel
    share = dirs // 2
    levels = n_basis // 4
    others = max(levels - 1, 1)
    group_w = 2 * panel
    cfg = (n_basis, n_ex, n_panels, half_rows, pad_rows, in_w, go_w, go_pad, tok, dirs)
    bf16, f32 = jnp.bfloat16, jnp.float32
    dma = pltpu.SemaphoreType.DMA
    quarter = pltpu.VMEM((n_panels, panel, pad_rows // 4), bf16)
    scratch = [
        pltpu.VMEM((n_panels, pad_rows, panel), bf16),
        pltpu.VMEM((go_pad, dirs), bf16),
        pltpu.VMEM((dirs, go_pad), bf16),
        pltpu.VMEM((n_ex, act_rows, tok), bf16),
        pltpu.VMEM((n_ex, go_pad, tok), bf16),
        pltpu.VMEM((width, pad_rows), bf16),
        pltpu.VMEM((2, width, pad_rows), bf16),
        pltpu.VMEM((n_ex, group_w, tok), f32),
        pltpu.VMEM((n_ex, dirs, tok), bf16),
        pltpu.VMEM((n_ex, width, tok), bf16),
        pltpu.VMEM((n_ex, dirs, width), f32),
        pltpu.VMEM((n_ex, share, width), f32),
        pltpu.VMEM((n_panels, panel, pad_rows // 2), bf16),
        quarter, quarter, quarter, quarter, quarter, quarter,
        pltpu.VMEM((2, share, group_w), f32),
        pltpu.VMEM((2, 3, share // 4, group_w), f32),
        pltpu.VMEM((2, share // 4, group_w), f32),
        pltpu.VMEM((2, others, share // 4, group_w), f32),
        pltpu.VMEM((2, share, group_w), f32),
        pltpu.VMEM((3, 8, LANE), f32),
        pltpu.VMEM((8, LANE), f32),
        pltpu.VMEM((3, 8, LANE), f32),
        pltpu.VMEM((others, 8, LANE), f32),
    ]
    scratch += [dma((n_panels,)), dma, dma((n_ex,)), dma((n_ex,))]
    scratch += [dma((n_panels, 2))] * 4 + [dma((n_panels, 3))] * 2 + [dma((n_panels,))] * 4
    scratch += [dma((2, n_ex))] * 2 + [dma((2, 3))] * 2 + [dma((2, others))] * 2 + [dma((2, 3))] * 2
    scratch += [dma] * 2 + [dma((3,))] * 2 + [dma((others,))] * 2
    smem = pl.BlockSpec(memory_space=pltpu.SMEM)
    anywhere = pl.BlockSpec(memory_space=pl.ANY)
    return pl.pallas_call(
        functools.partial(kernel, cfg),
        out_shape=jax.ShapeDtypeStruct((2 * n_ex, share, width), f32),
        in_specs=[smem, smem, anywhere, anywhere, anywhere, anywhere],
        out_specs=pl.BlockSpec(memory_space=pltpu.VMEM),
        scratch_shapes=scratch,
        compiler_params=pltpu.CompilerParams(
            collective_id=0, has_side_effects=True, vmem_limit_bytes=60 * 1024 * 1024),
        name="ekfac",
    )(owners, token_count, panel_store, grad_basis,
      jnp.swapaxes(activations, 1, 2), jnp.swapaxes(out_grads, 1, 2))


def solution(mesh):
    return jax.shard_map(
        per_device,
        mesh=mesh,
        in_specs=(
            P(("basis", "ex"), None, None),
            P(("basis", "ex"), None, None),
            P(),
            P("basis", None, "ex", None),
            P(),
            P(("basis", "ex")),
        ),
        out_specs=P("basis", "ex", None),
        check_vma=False,
    )
```
